32 devices in a mesh: parts: 2 (over y), mp: 4 (over z), dp: 4 (over x, core).
Axes of the slice: x: 2, y: 2, z: 4, core: 2. Of those that a mesh axis runs over, the one named last changes fastest.
Arguments:
- embeddings: bfloat16 [2048, 1024], P(('parts', 'dp')), parts along dimension 0, may hold values from -16 to 16
- w_in: bfloat16 [1024, 8192], P(None, 'mp'), may hold values from -0.1875 to 0.1875
- w_out: bfloat16 [8192, 1024], P('mp'), may hold values from -0.0625 to 0.0625
- means: bfloat16 [8192, 1024], P('mp'), may hold values from -2.09375 to 2.09375
- precisions: bfloat16 [8192, 1024], P('mp'), may hold values from 0.04 to 0.16
- log_weight: float32 [8192], P('mp'), may hold values from -4 to 0
Outputs:
- counts: float32 [16384], P(('parts', 'mp')), parts along dimension 0
- first_moment: float32 [2048, 8192], P(('parts', 'dp'), 'mp'), parts along dimension 0
- second_moment: float32 [2048, 8192], P(('parts', 'dp'), 'mp'), parts along dimension 0
- grad_w_in: bfloat16 [2048, 8192], P(('parts', 'dp'), 'mp'), parts along dimension 0
- grad_w_out_t: bfloat16 [2048, 8192], P(('parts', 'dp'), 'mp'), parts along dimension 0
- grad_embed: bfloat16 [2048, 1024], P(('parts', 'dp')), parts along dimension 0
The draws below stay inside these ranges and needn't reach their ends.
There are 2 independent parts, one for each index of `parts`. The reference program is written for one: setup_inputs(seed, part) draws one part's arguments, and reference() takes and returns one part's arrays. A program takes and returns all parts, laid end to end along the dimension named above; an argument that names none is the same for every part. Nothing has to cross between parts.
All inputs are finite; a program needn't handle non-finite values.
Results may differ from the reference program's by a relative error of at most 0.028.
Values may be sent and summed in bfloat16 or wider, within the bound.
A program may use at most 128 MiB of HBM per device.

```python
import math
import jax
import jax.numpy as jnp

D = 1024
H = 8192
K = 8192
R_DEV = 256
ROWS = 1024
N_DP = 4


def draw_embeddings(key, part):
    key_base = jax.random.fold_in(key, 11)
    key_scale = jax.random.fold_in(key, 12)
    base = jax.random.normal(key_base, (ROWS, D), jnp.float32)
    scale = jnp.exp(jax.random.uniform(key_scale, (ROWS, 1), jnp.float32, 0.0, math.log(4.0)))
    values = base * scale
    return jnp.clip(values, -16.0, 16.0).astype(jnp.bfloat16)


def draw_precisions(key, part):
    key_level = jax.random.fold_in(key, 21)
    key_spread = jax.random.fold_in(key, 22)
    level = jax.random.uniform(key_level, (K, 1), jnp.float32, -4.0 / D, 4.0 / D)
    spread = jax.random.uniform(key_spread, (K, D), jnp.float32, -0.35, 0.35)
    spread = spread - jnp.mean(spread, axis=1, keepdims=True)
    values = 0.08 * jnp.exp(level + spread)
    return jnp.clip(values, 0.0401, 0.159).astype(jnp.bfloat16)


def shard_levels(key, shape, pieces, smallest, high):
    level, own = 1.0, jax.random.fold_in(key, 6)
    for dim, parts in pieces:
        steps = jnp.exp(jax.random.uniform(jax.random.fold_in(own, dim), (parts,), jnp.float32, smallest / len(pieces), high / len(pieces)))
        level = level * jnp.repeat(steps, shape[dim] // parts).reshape([-1 if axis == dim else 1 for axis in range(len(shape))])
    return level


def bell_draw(stream_key, dims, width, bound, pieces=(), dtype=jnp.bfloat16):
    result = jax.random.normal(stream_key, dims, jnp.float32) * width
    if len(pieces) > 0:
        result = shard_levels(stream_key, dims, pieces, -0.22, 0.18) * result
    return jnp.clip(result, min=-bound, max=bound).astype(dtype)


def setup_inputs(seed: int = 0, part: int = 0) -> dict:
    seeds = jax.random.split(jax.random.key(seed), 7)
    part_keys = jax.random.split(jax.random.fold_in(seeds[6], part), 7)
    return {
        "embeddings": draw_embeddings(jax.random.fold_in(jax.random.fold_in(seeds[6], part), 71), part),
        "w_in": bell_draw(seeds[1], (D, H), D ** -0.5, 0.1875, ((1, 4),)),
        "w_out": bell_draw(seeds[2], (H, D), H ** -0.5, 0.0625, ((0, 4),)),
        "means": bell_draw(seeds[3], (K, D), 0.35, 2.09375, ((0, 4),)),
        "precisions": draw_precisions(jax.random.fold_in(seeds[6], 71), part),
        "log_weight": jnp.clip(-4.0 + 4.0 * jax.random.uniform(seeds[5], (K,), jnp.float32) ** shard_levels(seeds[5], (K,), ((0, 4),), -0.2, 0.2), -4.0, 0.0),
    }


def reference(embeddings, w_in, w_out, means, precisions, log_weight):
    pre = jnp.dot(embeddings, w_in, preferred_element_type=jnp.float32)
    hidden = jax.nn.silu(pre).astype(jnp.bfloat16)
    head = jnp.dot(hidden, w_out, preferred_element_type=jnp.float32).astype(jnp.bfloat16)
    head_f = head.astype(jnp.float32)
    squares = (head_f * head_f).astype(jnp.bfloat16)
    means_f = means.astype(jnp.float32)
    prec_f = precisions.astype(jnp.float32)
    weighted = (means_f * prec_f).astype(jnp.bfloat16)
    offset = log_weight + 0.5 * jnp.sum(jnp.log(prec_f), axis=1) - 0.5 * jnp.sum(means_f * means_f * prec_f, axis=1)
    scores = offset[None, :] + jnp.dot(head, weighted.T, preferred_element_type=jnp.float32) - 0.5 * jnp.dot(squares, precisions.T, preferred_element_type=jnp.float32)
    top = jnp.max(scores, axis=1)
    lse = top + jnp.log(jnp.sum(jnp.exp(scores - top[:, None]), axis=1))
    resp = jnp.exp(scores - lse[:, None])
    resp_b = resp.astype(jnp.bfloat16)
    counts = jnp.sum(resp, axis=0)
    first_moment = jnp.dot(head.T, resp_b, preferred_element_type=jnp.float32)
    second_moment = jnp.dot(squares.T, resp_b, preferred_element_type=jnp.float32)
    along = jnp.dot(resp_b, precisions, preferred_element_type=jnp.float32)
    shifted = jnp.dot(resp_b, weighted, preferred_element_type=jnp.float32)
    grad_head = (head_f * along - shifted).astype(jnp.bfloat16)
    back = jnp.dot(grad_head, w_out.T, preferred_element_type=jnp.float32)
    sigma = jax.nn.sigmoid(pre)
    grad_pre = (back * sigma * (1.0 + pre * (1.0 - sigma))).astype(jnp.bfloat16)
    grad_embed = jnp.dot(grad_pre, w_in.T, preferred_element_type=jnp.float32).astype(jnp.bfloat16)
    total_in = jnp.zeros((D, H), jnp.float32)
    total_out = jnp.zeros((D, H), jnp.float32)
    for block in range(N_DP):
        lower = block * R_DEV
        emb_blk = embeddings[lower:lower + R_DEV]
        pre_blk = grad_pre[lower:lower + R_DEV]
        grad_blk = grad_head[lower:lower + R_DEV]
        hid_blk = hidden[lower:lower + R_DEV]
        part_in = jnp.dot(emb_blk.T, pre_blk, preferred_element_type=jnp.float32).astype(jnp.bfloat16)
        part_out = jnp.dot(grad_blk.T, hid_blk, preferred_element_type=jnp.float32).astype(jnp.bfloat16)
        total_in = total_in + part_in.astype(jnp.float32)
        total_out = total_out + part_out.astype(jnp.float32)
    return (counts, first_moment, second_moment, total_in.astype(jnp.bfloat16), total_out.astype(jnp.bfloat16), grad_embed)
```

```python
import jax
import jax.numpy as jnp
from jax import lax
from jax.sharding import PartitionSpec as P


def my_columns(rows, axis):
    gathered = lax.all_gather(rows, axis, axis=0, tiled=True)
    width = rows.shape[1] // lax.axis_size(axis)
    return lax.dynamic_slice_in_dim(gathered, lax.axis_index(axis) * width, width, 1)


def body(embeddings, w_in, w_out, means, precisions, log_weight):
    contract_rows = (((0,), (0,)), ((), ()))
    contract_cols = (((1,), (1,)), ((), ()))
    pre = jnp.dot(embeddings, w_in, preferred_element_type=jnp.float32)
    hidden = jax.nn.silu(pre).astype(jnp.bfloat16)
    hidden_all = lax.all_gather(hidden, "dp", axis=0, tiled=True)
    emb_cols = my_columns(embeddings, "dp")
    partial_value = jnp.dot(hidden, w_out, preferred_element_type=jnp.float32)
    head = lax.psum(partial_value, "mp").astype(jnp.bfloat16)
    head_f = head.astype(jnp.float32)
    squares = (head_f * head_f).astype(jnp.bfloat16)
    means_f = means.astype(jnp.float32)
    prec_f = precisions.astype(jnp.float32)
    weighted = (means_f * prec_f).astype(jnp.bfloat16)
    offset = (
        log_weight
        + 0.5 * jnp.sum(jnp.log(prec_f), axis=1)
        - 0.5 * jnp.sum(means_f * means_f * prec_f, axis=1)
    )
    scores = offset[None, :] + lax.dot_general(
        head, weighted, contract_cols, preferred_element_type=jnp.float32
    )
    scores = scores - 0.5 * lax.dot_general(
        squares, precisions, contract_cols, preferred_element_type=jnp.float32
    )
    local_top = jnp.max(scores, axis=1)
    local_total = jnp.sum(jnp.exp(scores - local_top[:, None]), axis=1)
    stats = lax.all_gather(jnp.stack([local_top, local_total]), "mp")
    top = jnp.max(stats[:, 0], axis=0)
    total = jnp.sum(stats[:, 1] * jnp.exp(stats[:, 0] - top), axis=0)
    lse = top + jnp.log(total)
    resp = jnp.exp(scores - lse[:, None])
    resp_b = resp.astype(jnp.bfloat16)
    counts = lax.psum(jnp.sum(resp, axis=0), "dp")
    resp_all = lax.all_gather(resp_b, "dp", axis=0, tiled=True)
    head_cols = my_columns(head, "dp")
    head_cols_f = head_cols.astype(jnp.float32)
    squares_cols = (head_cols_f * head_cols_f).astype(jnp.bfloat16)
    first_moment = lax.dot_general(
        head_cols, resp_all, contract_rows, preferred_element_type=jnp.float32
    )
    second_moment = lax.dot_general(
        squares_cols, resp_all, contract_rows, preferred_element_type=jnp.float32
    )
    along = jnp.dot(resp_b, precisions, preferred_element_type=jnp.float32)
    shifted = jnp.dot(resp_b, weighted, preferred_element_type=jnp.float32)
    grad_term = head_f * along - shifted
    grad_head = lax.psum(grad_term.astype(jnp.bfloat16), "mp")
    back = lax.dot_general(grad_head, w_out, contract_cols, preferred_element_type=jnp.float32)
    sigma = jax.nn.sigmoid(pre)
    grad_pre = (back * sigma * (1.0 + pre * (1.0 - sigma))).astype(jnp.bfloat16)
    embed_term = lax.dot_general(grad_pre, w_in, contract_cols, preferred_element_type=jnp.float32)
    grad_embed = lax.psum(embed_term.astype(jnp.bfloat16), "mp")
    pre_all = lax.all_gather(grad_pre, "dp", axis=0, tiled=True)
    grad_cols = my_columns(grad_head, "dp")
    grad_w_in = lax.dot_general(
        emb_cols, pre_all, contract_rows, preferred_element_type=jnp.float32
    ).astype(jnp.bfloat16)
    grad_w_out_t = lax.dot_general(
        grad_cols, hidden_all, contract_rows, preferred_element_type=jnp.float32
    ).astype(jnp.bfloat16)
    return (counts, first_moment, second_moment, grad_w_in, grad_w_out_t, grad_embed)


def solution(mesh):
    return jax.shard_map(
        body,
        mesh=mesh,
        in_specs=(
            P(("parts", "dp"), None),
            P(None, "mp"),
            P("mp", None),
            P("mp", None),
            P("mp", None),
            P("mp"),
        ),
        out_specs=(
            P(("parts", "mp")),
            P(("parts", "dp"), "mp"),
            P(("parts", "dp"), "mp"),
            P(("parts", "dp"), "mp"),
            P(("parts", "dp"), "mp"),
            P(("parts", "dp"), None),
        ),
        check_vma=False,
    )
```

```python
import functools

import jax
import jax.numpy as jnp
from jax import lax
from jax.experimental import pallas as pl
from jax.experimental.pallas import tpu as pltpu
from jax.sharding import PartitionSpec as P


def send(src, dst, send_sem, recv_sem, axis, peer):
    return pltpu.make_async_remote_copy(
        src_ref=src,
        dst_ref=dst,
        send_sem=send_sem,
        recv_sem=recv_sem,
        device_id={axis: peer},
        device_id_type=pl.DeviceIdType.MESH,
    )


def greet(groups):
    barrier = pltpu.get_barrier_semaphore()
    count = 0
    for axis, size in groups:
        me = lax.axis_index(axis)
        for step in range(1, size):
            pl.semaphore_signal(
                barrier,
                inc=1,
                device_id={axis: lax.rem(me + step, size)},
                device_id_type=pl.DeviceIdType.MESH,
            )
            count += 1
    pl.semaphore_wait(barrier, count)


def stats_kernel(n, in_ref, out_ref, send_sem, recv_sem):
    greet((("mp", n),))
    me = lax.axis_index("mp")
    copies = []
    for step in range(1, n):
        peer = lax.rem(me + step, n)
        copies.append(
            send(in_ref, out_ref.at[me], send_sem.at[step], recv_sem.at[step], "mp", peer)
        )
        copies[-1].start()
    out_ref[me] = in_ref[...]
    for step in range(1, n):
        copies[step - 1].wait_send()
        source = lax.rem(me + n - step, n)
        send(
            in_ref, out_ref.at[source], send_sem.at[step], recv_sem.at[step], "mp", source
        ).wait_recv()


def gather_stats(stats, n, collective_id):
    return pl.pallas_call(
        functools.partial(stats_kernel, n),
        out_shape=jax.ShapeDtypeStruct((n,) + stats.shape, stats.dtype),
        in_specs=[pl.BlockSpec(memory_space=pltpu.VMEM)],
        out_specs=pl.BlockSpec(memory_space=pltpu.VMEM),
        scratch_shapes=[pltpu.SemaphoreType.DMA((n,)), pltpu.SemaphoreType.DMA((n,))],
        compiler_params=pltpu.CompilerParams(
            collective_id=collective_id, has_side_effects=True, vmem_limit_bytes=4 << 20
        ),
    )(stats)


def exchange_kernel(n_mp, n_dp, pieces, term, block, wide, vec, *refs):
    (total, gathered, columns, vecs, landed) = refs[:5]
    (sum_s, sum_r, out_s, out_r, col_s, col_r, vec_s, vec_r) = refs[5:13]
    (pair_s, pair_r, far_s, far_r, fwd_s, fwd_r, own_sem) = refs[13:]
    greet((("mp", n_mp), ("dp", n_dp)))
    me, dp = lax.axis_index("mp"), lax.axis_index("dp")
    n_x = n_dp // 2
    core, x = lax.rem(dp, 2), lax.div(dp, 2)
    partner = 2 * x + 1 - core
    rows = block.shape[0]
    piece = rows // pieces
    width = wide.shape[1] // n_dp
    sent = []

    def go(*args):
        copy = send(*args)
        copy.start()
        sent.append(copy)

    def arrived(dst, send_sem, recv_sem, axis, peer):
        send(dst, dst, send_sem, recv_sem, axis, peer).wait_recv()

    for step in range(1, n_mp):
        peer = lax.rem(me + step, n_mp)
        go(term.at[peer], landed.at[step], sum_s.at[step], sum_r.at[step], "mp", peer)
    for far in range(1, n_x):
        peer = 2 * lax.rem(x + far, n_x) + core
        for g in range(pieces):
            part = pl.ds(g * piece, piece)
            go(
                block.at[part],
                gathered.at[dp, part],
                far_s.at[far, g],
                far_r.at[far, g],
                "dp",
                peer,
            )
    go(block, gathered.at[dp], pair_s, pair_r, "dp", partner)
    for step in range(1, n_dp):
        peer = lax.rem(dp + step, n_dp)
        cols = pl.ds(pl.multiple_of(peer * width, width), width)
        go(wide.at[:, cols], columns.at[dp], col_s.at[step], col_r.at[step], "dp", peer)
        go(vec, vecs.at[dp], vec_s.at[step], vec_r.at[step], "dp", peer)
    cols = pl.ds(pl.multiple_of(dp * width, width), width)
    own = [
        pltpu.make_async_copy(block, gathered.at[dp], own_sem.at[0]),
        pltpu.make_async_copy(wide.at[:, cols], columns.at[dp], own_sem.at[1]),
        pltpu.make_async_copy(vec, vecs.at[dp], own_sem.at[2]),
    ]
    for copy in own:
        copy.start()

    acc = term[me].astype(jnp.float32)
    for step in range(1, n_mp):
        peer = lax.rem(me + step, n_mp)
        arrived(landed.at[step], sum_s.at[step], sum_r.at[step], "mp", peer)
        acc = acc + landed[step].astype(jnp.float32)
    total[me] = acc.astype(total.dtype)
    for step in range(1, n_mp):
        peer = lax.rem(me + step, n_mp)
        go(total.at[me], total.at[me], out_s.at[step], out_r.at[step], "mp", peer)

    for g in range(pieces):
        part = pl.ds(g * piece, piece)
        for far in range(1, n_x):
            source = 2 * lax.rem(x + n_x - far, n_x) + core
            spot = gathered.at[source, part]
            arrived(spot, far_s.at[far, g], far_r.at[far, g], "dp", source)
            go(spot, spot, fwd_s.at[far, g], fwd_r.at[far, g], "dp", partner)
    arrived(gathered.at[partner], pair_s, pair_r, "dp", partner)
    for step in range(1, n_dp):
        source = lax.rem(dp + n_dp - step, n_dp)
        arrived(columns.at[source], col_s.at[step], col_r.at[step], "dp", source)
        arrived(vecs.at[source], vec_s.at[step], vec_r.at[step], "dp", source)
    for g in range(pieces):
        part = pl.ds(g * piece, piece)
        for far in range(1, n_x):
            source = 2 * lax.rem(x + n_x - far, n_x) + 1 - core
            arrived(
                gathered.at[source, part], fwd_s.at[far, g], fwd_r.at[far, g], "dp", partner
            )
    for step in range(1, n_mp):
        source = lax.rem(me + n_mp - step, n_mp)
        arrived(total.at[source], out_s.at[step], out_r.at[step], "mp", source)
    for copy in own:
        copy.wait()
    for copy in sent:
        copy.wait_send()


def exchange(term, block, wide, vec, n_mp, n_dp, collective_id):
    pieces = 4 if block.shape[0] % 64 == 0 else 1
    rows, width = wide.shape[0], wide.shape[1] // n_dp
    dma = pltpu.SemaphoreType.DMA
    chunk = (n_mp, term.shape[0] // n_mp, term.shape[1])
    vmem = pl.BlockSpec(memory_space=pltpu.VMEM)
    total, gathered, columns, vecs = pl.pallas_call(
        functools.partial(exchange_kernel, n_mp, n_dp, pieces),
        out_shape=(
            jax.ShapeDtypeStruct(chunk, term.dtype),
            jax.ShapeDtypeStruct((n_dp,) + block.shape, block.dtype),
            jax.ShapeDtypeStruct((n_dp, rows, width), wide.dtype),
            jax.ShapeDtypeStruct((n_dp,) + vec.shape, vec.dtype),
        ),
        in_specs=[vmem] * 4,
        out_specs=(vmem,) * 4,
        scratch_shapes=[
            pltpu.VMEM(chunk, term.dtype),
            dma((n_mp,)),
            dma((n_mp,)),
            dma((n_mp,)),
            dma((n_mp,)),
            dma((n_dp,)),
            dma((n_dp,)),
            dma((n_dp,)),
            dma((n_dp,)),
            dma,
            dma,
            dma((n_dp // 2, pieces)),
            dma((n_dp // 2, pieces)),
            dma((n_dp // 2, pieces)),
            dma((n_dp // 2, pieces)),
            dma((3,)),
        ],
        compiler_params=pltpu.CompilerParams(
            collective_id=collective_id, has_side_effects=True, vmem_limit_bytes=20 << 20
        ),
    )(term.reshape(chunk), block, wide, vec)
    return (
        total.reshape(term.shape),
        gathered.reshape(n_dp * block.shape[0], block.shape[1]),
        columns.reshape(n_dp * rows, width),
        vecs,
    )


def body(n_mp, n_dp, embeddings, w_in, w_out, means, precisions, log_weight):
    contract_rows = (((0,), (0,)), ((), ()))
    contract_cols = (((1,), (1,)), ((), ()))
    pre = jnp.dot(embeddings, w_in, preferred_element_type=jnp.float32)
    hidden = jax.nn.silu(pre).astype(jnp.bfloat16)
    partial_value = jnp.dot(hidden, w_out, preferred_element_type=jnp.float32)
    spare = jnp.zeros((1, 128), jnp.float32)
    head, hidden_all, emb_cols, _ = exchange(
        partial_value.astype(jnp.bfloat16), hidden, embeddings, spare, n_mp, n_dp, 0
    )
    head_f = head.astype(jnp.float32)
    squares = (head_f * head_f).astype(jnp.bfloat16)
    means_f = means.astype(jnp.float32)
    prec_f = precisions.astype(jnp.float32)
    weighted = (means_f * prec_f).astype(jnp.bfloat16)
    offset = (
        log_weight
        + 0.5 * jnp.sum(jnp.log(prec_f), axis=1)
        - 0.5 * jnp.sum(means_f * means_f * prec_f, axis=1)
    )
    scores = offset[None, :] + lax.dot_general(
        head, weighted, contract_cols, preferred_element_type=jnp.float32
    )
    scores = scores - 0.5 * lax.dot_general(
        squares, precisions, contract_cols, preferred_element_type=jnp.float32
    )
    local_top = jnp.max(scores, axis=1)
    local_total = jnp.sum(jnp.exp(scores - local_top[:, None]), axis=1)
    stats = gather_stats(jnp.stack([local_top, local_total]), n_mp, 1)
    top = jnp.max(stats[:, 0], axis=0)
    total = jnp.sum(stats[:, 1] * jnp.exp(stats[:, 0] - top), axis=0)
    lse = top + jnp.log(total)
    resp = jnp.exp(scores - lse[:, None])
    resp_b = resp.astype(jnp.bfloat16)
    along = jnp.dot(resp_b, precisions, preferred_element_type=jnp.float32)
    shifted = jnp.dot(resp_b, weighted, preferred_element_type=jnp.float32)
    grad_term = head_f * along - shifted
    grad_head, resp_all, head_cols, counts_all = exchange(
        grad_term.astype(jnp.bfloat16),
        resp_b,
        head,
        jnp.sum(resp, axis=0, keepdims=True),
        n_mp,
        n_dp,
        2,
    )
    counts = jnp.sum(counts_all, axis=(0, 1))
    head_cols_f = head_cols.astype(jnp.float32)
    squares_cols = (head_cols_f * head_cols_f).astype(jnp.bfloat16)
    first_moment = lax.dot_general(
        head_cols, resp_all, contract_rows, preferred_element_type=jnp.float32
    )
    second_moment = lax.dot_general(
        squares_cols, resp_all, contract_rows, preferred_element_type=jnp.float32
    )
    back = lax.dot_general(grad_head, w_out, contract_cols, preferred_element_type=jnp.float32)
    sigma = jax.nn.sigmoid(pre)
    grad_pre = (back * sigma * (1.0 + pre * (1.0 - sigma))).astype(jnp.bfloat16)
    embed_term = lax.dot_general(grad_pre, w_in, contract_cols, preferred_element_type=jnp.float32)
    grad_embed, pre_all, grad_cols, _ = exchange(
        embed_term.astype(jnp.bfloat16), grad_pre, grad_head, spare, n_mp, n_dp, 3
    )
    grad_w_in = lax.dot_general(
        emb_cols, pre_all, contract_rows, preferred_element_type=jnp.float32
    ).astype(jnp.bfloat16)
    grad_w_out_t = lax.dot_general(
        grad_cols, hidden_all, contract_rows, preferred_element_type=jnp.float32
    ).astype(jnp.bfloat16)
    return (counts, first_moment, second_moment, grad_w_in, grad_w_out_t, grad_embed)


def solution(mesh):
    return jax.shard_map(
        functools.partial(body, mesh.shape["mp"], mesh.shape["dp"]),
        mesh=mesh,
        in_specs=(
            P(("parts", "dp"), None),
            P(None, "mp"),
            P("mp", None),
            P("mp", None),
            P("mp", None),
            P("mp"),
        ),
        out_specs=(
            P(("parts", "mp")),
            P(("parts", "dp"), "mp"),
            P(("parts", "dp"), "mp"),
            P(("parts", "dp"), "mp"),
            P(("parts", "dp"), "mp"),
            P(("parts", "dp"), None),
        ),
        check_vma=False,
    )
```

```python
import functools
import math

import jax
import jax.numpy as jnp
from jax import lax
from jax.experimental import pallas as pl
from jax.experimental.pallas import tpu as pltpu
from jax.sharding import PartitionSpec as P


def send(src, dst, send_sem, recv_sem, axis, peer):
    return pltpu.make_async_remote_copy(
        src_ref=src,
        dst_ref=dst,
        send_sem=send_sem,
        recv_sem=recv_sem,
        device_id={axis: peer},
        device_id_type=pl.DeviceIdType.MESH,
    )


def greet(groups):
    barrier = pltpu.get_barrier_semaphore()
    count = 0
    for axis, size in groups:
        me = lax.axis_index(axis)
        for step in range(1, size):
            pl.semaphore_signal(
                barrier,
                inc=1,
                device_id={axis: lax.rem(me + step, size)},
                device_id_type=pl.DeviceIdType.MESH,
            )
            count += 1
    pl.semaphore_wait(barrier, count)


def stats_kernel(n, in_ref, out_ref, send_sem, recv_sem):
    greet((("mp", n),))
    me = lax.axis_index("mp")
    copies = []
    for step in range(1, n):
        peer = lax.rem(me + step, n)
        copies.append(
            send(in_ref, out_ref.at[me], send_sem.at[step], recv_sem.at[step], "mp", peer)
        )
        copies[-1].start()
    out_ref[me] = in_ref[...]
    for step in range(1, n):
        copies[step - 1].wait_send()
        source = lax.rem(me + n - step, n)
        send(
            in_ref, out_ref.at[source], send_sem.at[step], recv_sem.at[step], "mp", source
        ).wait_recv()


def gather_stats(stats, n, collective_id):
    return pl.pallas_call(
        functools.partial(stats_kernel, n),
        out_shape=jax.ShapeDtypeStruct((n,) + stats.shape, stats.dtype),
        in_specs=[pl.BlockSpec(memory_space=pltpu.VMEM)],
        out_specs=pl.BlockSpec(memory_space=pltpu.VMEM),
        scratch_shapes=[pltpu.SemaphoreType.DMA((n,)), pltpu.SemaphoreType.DMA((n,))],
        compiler_params=pltpu.CompilerParams(
            collective_id=collective_id, has_side_effects=True, vmem_limit_bytes=4 << 20
        ),
    )(stats)


def offset_side(means, precisions, out):
    tile = math.gcd(means.shape[0], 64)
    depth = means.shape[1]
    lanes = out.shape[1]

    def step(i, carry):
        rows = pl.ds(pl.multiple_of(i * tile, tile), tile)
        acc = jnp.zeros((tile, lanes), jnp.float32)
        for col in range(0, depth, lanes):
            mean = means[rows, col : col + lanes].astype(jnp.float32)
            prec = precisions[rows, col : col + lanes].astype(jnp.float32)
            acc = acc + (jnp.log(prec) - mean * mean * prec)
        out[rows, :] = 0.5 * acc
        return carry

    lax.fori_loop(0, means.shape[0] // tile, step, 0)


def moment_side(feats, resp, first, second):
    tile = math.gcd(resp.shape[1], 256)
    half = first.shape[0]

    def step(i, carry):
        cols = pl.ds(pl.multiple_of(i * tile, tile), tile)
        value = jnp.dot(feats[...], resp[:, cols], preferred_element_type=jnp.float32)
        first[:, cols] = value[:half]
        second[:, cols] = value[half:]
        return carry

    lax.fori_loop(0, resp.shape[1] // tile, step, 0)


def exchange_kernel(n_mp, n_dp, pieces, side, n_in, n_out, term, block, wide, vec, *refs):
    side_in, refs = refs[:n_in], refs[n_in:]
    (total, gathered, columns, vecs), refs = refs[:4], refs[4:]
    side_out, refs = refs[:n_out], refs[n_out:]
    landed = refs[0]
    (sum_s, sum_r, out_s, out_r, col_s, col_r, vec_s, vec_r) = refs[1:9]
    (pair_s, pair_r, far_s, far_r, fwd_s, fwd_r, own_sem) = refs[9:]
    greet((("mp", n_mp), ("dp", n_dp)))
    me, dp = lax.axis_index("mp"), lax.axis_index("dp")
    n_x = n_dp // 2
    core, x = lax.rem(dp, 2), lax.div(dp, 2)
    partner = 2 * x + 1 - core
    rows = block.shape[0]
    piece = rows // pieces
    width = wide.shape[1] // n_dp
    sent = []

    def go(*args):
        copy = send(*args)
        copy.start()
        sent.append(copy)

    def arrived(dst, send_sem, recv_sem, axis, peer):
        send(dst, dst, send_sem, recv_sem, axis, peer).wait_recv()

    for step in range(1, n_mp):
        peer = lax.rem(me + step, n_mp)
        go(term.at[peer], landed.at[step], sum_s.at[step], sum_r.at[step], "mp", peer)
    for far in range(1, n_x):
        peer = 2 * lax.rem(x + far, n_x) + core
        for g in range(pieces):
            part = pl.ds(g * piece, piece)
            go(
                block.at[part],
                gathered.at[dp, part],
                far_s.at[far, g],
                far_r.at[far, g],
                "dp",
                peer,
            )
    go(block, gathered.at[dp], pair_s, pair_r, "dp", partner)
    for step in range(1, n_dp):
        peer = lax.rem(dp + step, n_dp)
        cols = pl.ds(pl.multiple_of(peer * width, width), width)
        go(wide.at[:, cols], columns.at[dp], col_s.at[step], col_r.at[step], "dp", peer)
        go(vec, vecs.at[dp], vec_s.at[step], vec_r.at[step], "dp", peer)
    cols = pl.ds(pl.multiple_of(dp * width, width), width)
    own = [
        pltpu.make_async_copy(block, gathered.at[dp], own_sem.at[0]),
        pltpu.make_async_copy(wide.at[:, cols], columns.at[dp], own_sem.at[1]),
        pltpu.make_async_copy(vec, vecs.at[dp], own_sem.at[2]),
    ]
    for copy in own:
        copy.start()

    if side is not None:
        side(*side_in, *side_out)

    acc = term[me].astype(jnp.float32)
    for step in range(1, n_mp):
        peer = lax.rem(me + step, n_mp)
        arrived(landed.at[step], sum_s.at[step], sum_r.at[step], "mp", peer)
        acc = acc + landed[step].astype(jnp.float32)
    total[me] = acc.astype(total.dtype)
    for step in range(1, n_mp):
        peer = lax.rem(me + step, n_mp)
        go(total.at[me], total.at[me], out_s.at[step], out_r.at[step], "mp", peer)

    for g in range(pieces):
        part = pl.ds(g * piece, piece)
        for far in range(1, n_x):
            source = 2 * lax.rem(x + n_x - far, n_x) + core
            spot = gathered.at[source, part]
            arrived(spot, far_s.at[far, g], far_r.at[far, g], "dp", source)
            go(spot, spot, fwd_s.at[far, g], fwd_r.at[far, g], "dp", partner)
    arrived(gathered.at[partner], pair_s, pair_r, "dp", partner)
    for step in range(1, n_dp):
        source = lax.rem(dp + n_dp - step, n_dp)
        arrived(columns.at[source], col_s.at[step], col_r.at[step], "dp", source)
        arrived(vecs.at[source], vec_s.at[step], vec_r.at[step], "dp", source)
    for g in range(pieces):
        part = pl.ds(g * piece, piece)
        for far in range(1, n_x):
            source = 2 * lax.rem(x + n_x - far, n_x) + 1 - core
            arrived(
                gathered.at[source, part], fwd_s.at[far, g], fwd_r.at[far, g], "dp", partner
            )
    for step in range(1, n_mp):
        source = lax.rem(me + n_mp - step, n_mp)
        arrived(total.at[source], out_s.at[step], out_r.at[step], "mp", source)
    for copy in own:
        copy.wait()
    for copy in sent:
        copy.wait_send()


def exchange(term, block, wide, vec, n_mp, n_dp, collective_id, side=None, side_in=(), side_out=()):
    pieces = 4 if block.shape[0] % 64 == 0 else 1
    rows, width = wide.shape[0], wide.shape[1] // n_dp
    dma = pltpu.SemaphoreType.DMA
    chunk = (n_mp, term.shape[0] // n_mp, term.shape[1])
    vmem = pl.BlockSpec(memory_space=pltpu.VMEM)
    total, gathered, columns, vecs, *extra = pl.pallas_call(
        functools.partial(exchange_kernel, n_mp, n_dp, pieces, side, len(side_in), len(side_out)),
        out_shape=(
            jax.ShapeDtypeStruct(chunk, term.dtype),
            jax.ShapeDtypeStruct((n_dp,) + block.shape, block.dtype),
            jax.ShapeDtypeStruct((n_dp, rows, width), wide.dtype),
            jax.ShapeDtypeStruct((n_dp,) + vec.shape, vec.dtype),
        )
        + tuple(side_out),
        in_specs=[vmem] * (4 + len(side_in)),
        out_specs=(vmem,) * (4 + len(side_out)),
        scratch_shapes=[
            pltpu.VMEM(chunk, term.dtype),
            dma((n_mp,)),
            dma((n_mp,)),
            dma((n_mp,)),
            dma((n_mp,)),
            dma((n_dp,)),
            dma((n_dp,)),
            dma((n_dp,)),
            dma((n_dp,)),
            dma,
            dma,
            dma((n_dp // 2, pieces)),
            dma((n_dp // 2, pieces)),
            dma((n_dp // 2, pieces)),
            dma((n_dp // 2, pieces)),
            dma((3,)),
        ],
        compiler_params=pltpu.CompilerParams(
            collective_id=collective_id, has_side_effects=True, vmem_limit_bytes=32 << 20
        ),
    )(term.reshape(chunk), block, wide, vec, *side_in)
    return (
        total.reshape(term.shape),
        gathered.reshape(n_dp * block.shape[0], block.shape[1]),
        columns.reshape(n_dp * rows, width),
        vecs,
        *extra,
    )


def body(n_mp, n_dp, embeddings, w_in, w_out, means, precisions, log_weight):
    contract_rows = (((0,), (0,)), ((), ()))
    contract_cols = (((1,), (1,)), ((), ()))
    pre = jnp.dot(embeddings, w_in, preferred_element_type=jnp.float32)
    hidden = jax.nn.silu(pre).astype(jnp.bfloat16)
    partial_value = jnp.dot(hidden, w_out, preferred_element_type=jnp.float32)
    spare = jnp.zeros((1, 128), jnp.float32)
    head, hidden_all, emb_cols, _, halves = exchange(
        partial_value.astype(jnp.bfloat16),
        hidden,
        embeddings,
        spare,
        n_mp,
        n_dp,
        0,
        offset_side,
        (means, precisions),
        (jax.ShapeDtypeStruct((means.shape[0], 128), jnp.float32),),
    )
    head_f = head.astype(jnp.float32)
    squares = (head_f * head_f).astype(jnp.bfloat16)
    means_f = means.astype(jnp.float32)
    prec_f = precisions.astype(jnp.float32)
    weighted = (means_f * prec_f).astype(jnp.bfloat16)
    offset = log_weight + jnp.sum(halves, axis=1)
    scores = offset[None, :] + lax.dot_general(
        head, weighted, contract_cols, preferred_element_type=jnp.float32
    )
    scores = scores - 0.5 * lax.dot_general(
        squares, precisions, contract_cols, preferred_element_type=jnp.float32
    )
    local_top = jnp.max(scores, axis=1)
    local_total = jnp.sum(jnp.exp(scores - local_top[:, None]), axis=1)
    stats = gather_stats(jnp.stack([local_top, local_total]), n_mp, 1)
    top = jnp.max(stats[:, 0], axis=0)
    total = jnp.sum(stats[:, 1] * jnp.exp(stats[:, 0] - top), axis=0)
    lse = top + jnp.log(total)
    resp = jnp.exp(scores - lse[:, None])
    resp_b = resp.astype(jnp.bfloat16)
    along = jnp.dot(resp_b, precisions, preferred_element_type=jnp.float32)
    shifted = jnp.dot(resp_b, weighted, preferred_element_type=jnp.float32)
    grad_term = head_f * along - shifted
    grad_head, resp_all, head_cols, counts_all = exchange(
        grad_term.astype(jnp.bfloat16),
        resp_b,
        head,
        jnp.sum(resp, axis=0, keepdims=True),
        n_mp,
        n_dp,
        2,
    )
    counts = jnp.sum(counts_all, axis=(0, 1))
    head_cols_f = head_cols.astype(jnp.float32)
    squares_cols = (head_cols_f * head_cols_f).astype(jnp.bfloat16)
    feats = jnp.concatenate([head_cols, squares_cols], axis=1).T
    moment = jax.ShapeDtypeStruct((head_cols.shape[1], resp_all.shape[1]), jnp.float32)
    back = lax.dot_general(grad_head, w_out, contract_cols, preferred_element_type=jnp.float32)
    sigma = jax.nn.sigmoid(pre)
    grad_pre = (back * sigma * (1.0 + pre * (1.0 - sigma))).astype(jnp.bfloat16)
    embed_term = lax.dot_general(grad_pre, w_in, contract_cols, preferred_element_type=jnp.float32)
    grad_embed, pre_all, grad_cols, _, first_moment, second_moment = exchange(
        embed_term.astype(jnp.bfloat16),
        grad_pre,
        grad_head,
        spare,
        n_mp,
        n_dp,
        3,
        moment_side,
        (feats, resp_all),
        (moment, moment),
    )
    grad_w_in = lax.dot_general(
        emb_cols, pre_all, contract_rows, preferred_element_type=jnp.float32
    ).astype(jnp.bfloat16)
    grad_w_out_t = lax.dot_general(
        grad_cols, hidden_all, contract_rows, preferred_element_type=jnp.float32
    ).astype(jnp.bfloat16)
    return (counts, first_moment, second_moment, grad_w_in, grad_w_out_t, grad_embed)


def solution(mesh):
    return jax.shard_map(
        functools.partial(body, mesh.shape["mp"], mesh.shape["dp"]),
        mesh=mesh,
        in_specs=(
            P(("parts", "dp"), None),
            P(None, "mp"),
            P("mp", None),
            P("mp", None),
            P("mp", None),
            P("mp"),
        ),
        out_specs=(
            P(("parts", "mp")),
            P(("parts", "dp"), "mp"),
            P(("parts", "dp"), "mp"),
            P(("parts", "dp"), "mp"),
            P(("parts", "dp"), "mp"),
            P(("parts", "dp"), None),
        ),
        check_vma=False,
    )
```

```python
import functools

import jax
import jax.numpy as jnp
from jax import lax
from jax.experimental import pallas as pl
from jax.experimental.pallas import tpu as pltpu
from jax.sharding import PartitionSpec as P


def send(src, dst, send_sem, recv_sem, axis, peer):
    return pltpu.make_async_remote_copy(
        src_ref=src,
        dst_ref=dst,
        send_sem=send_sem,
        recv_sem=recv_sem,
        device_id={axis: peer},
        device_id_type=pl.DeviceIdType.MESH,
    )


def greet(groups):
    barrier = pltpu.get_barrier_semaphore()
    count = 0
    for axis, size in groups:
        me = lax.axis_index(axis)
        for step in range(1, size):
            pl.semaphore_signal(
                barrier,
                inc=1,
                device_id={axis: lax.rem(me + step, size)},
                device_id_type=pl.DeviceIdType.MESH,
            )
            count += 1
    pl.semaphore_wait(barrier, count)


def stats_kernel(n, in_ref, out_ref, send_sem, recv_sem):
    greet((("mp", n),))
    me = lax.axis_index("mp")
    copies = []
    for step in range(1, n):
        peer = lax.rem(me + step, n)
        copies.append(
            send(in_ref, out_ref.at[me], send_sem.at[step], recv_sem.at[step], "mp", peer)
        )
        copies[-1].start()
    out_ref[me] = in_ref[...]
    for step in range(1, n):
        copies[step - 1].wait_send()
        source = lax.rem(me + n - step, n)
        send(
            in_ref, out_ref.at[source], send_sem.at[step], recv_sem.at[step], "mp", source
        ).wait_recv()


def gather_stats(stats, n, collective_id):
    return pl.pallas_call(
        functools.partial(stats_kernel, n),
        out_shape=jax.ShapeDtypeStruct((n,) + stats.shape, stats.dtype),
        in_specs=[pl.BlockSpec(memory_space=pltpu.VMEM)],
        out_specs=pl.BlockSpec(memory_space=pltpu.VMEM),
        scratch_shapes=[pltpu.SemaphoreType.DMA((n,)), pltpu.SemaphoreType.DMA((n,))],
        compiler_params=pltpu.CompilerParams(
            collective_id=collective_id, has_side_effects=True, vmem_limit_bytes=4 << 20
        ),
    )(stats)


def exchange_kernel(n_mp, n_dp, pieces, term, block, wide, vec, *refs):
    (total, gathered, columns, vecs, landed) = refs[:5]
    (sum_s, sum_r, out_s, out_r, col_s, col_r, vec_s, vec_r) = refs[5:13]
    (pair_s, pair_r, far_s, far_r, fwd_s, fwd_r, own_sem) = refs[13:]
    greet((("mp", n_mp), ("dp", n_dp)))
    me, dp = lax.axis_index("mp"), lax.axis_index("dp")
    n_x = n_dp // 2
    core, x = lax.rem(dp, 2), lax.div(dp, 2)
    partner = 2 * x + 1 - core
    rows = block.shape[0]
    piece = rows // pieces
    width = wide.shape[1] // n_dp
    sent = []

    def go(*args):
        copy = send(*args)
        copy.start()
        sent.append(copy)

    def arrived(dst, send_sem, recv_sem, axis, peer):
        send(dst, dst, send_sem, recv_sem, axis, peer).wait_recv()

    for step in range(1, n_mp):
        peer = lax.rem(me + step, n_mp)
        go(term.at[peer], landed.at[step], sum_s.at[step], sum_r.at[step], "mp", peer)
    for far in range(1, n_x):
        peer = 2 * lax.rem(x + far, n_x) + core
        for g in range(pieces):
            part = pl.ds(g * piece, piece)
            go(
                block.at[part],
                gathered.at[dp, part],
                far_s.at[far, g],
                far_r.at[far, g],
                "dp",
                peer,
            )
    go(block, gathered.at[dp], pair_s, pair_r, "dp", partner)
    for step in range(1, n_dp):
        peer = lax.rem(dp + step, n_dp)
        cols = pl.ds(pl.multiple_of(peer * width, width), width)
        go(wide.at[:, cols], columns.at[dp], col_s.at[step], col_r.at[step], "dp", peer)
        go(vec, vecs.at[dp], vec_s.at[step], vec_r.at[step], "dp", peer)
    cols = pl.ds(pl.multiple_of(dp * width, width), width)
    own = [
        pltpu.make_async_copy(block, gathered.at[dp], own_sem.at[0]),
        pltpu.make_async_copy(wide.at[:, cols], columns.at[dp], own_sem.at[1]),
        pltpu.make_async_copy(vec, vecs.at[dp], own_sem.at[2]),
    ]
    for copy in own:
        copy.start()

    acc = term[me].astype(jnp.float32)
    for step in range(1, n_mp):
        peer = lax.rem(me + step, n_mp)
        arrived(landed.at[step], sum_s.at[step], sum_r.at[step], "mp", peer)
        acc = acc + landed[step].astype(jnp.float32)
    total[me] = acc.astype(total.dtype)
    for step in range(1, n_mp):
        peer = lax.rem(me + step, n_mp)
        go(total.at[me], total.at[me], out_s.at[step], out_r.at[step], "mp", peer)

    for g in range(pieces):
        part = pl.ds(g * piece, piece)
        for far in range(1, n_x):
            source = 2 * lax.rem(x + n_x - far, n_x) + core
            spot = gathered.at[source, part]
            arrived(spot, far_s.at[far, g], far_r.at[far, g], "dp", source)
            go(spot, spot, fwd_s.at[far, g], fwd_r.at[far, g], "dp", partner)
    arrived(gathered.at[partner], pair_s, pair_r, "dp", partner)
    for step in range(1, n_dp):
        source = lax.rem(dp + n_dp - step, n_dp)
        arrived(columns.at[source], col_s.at[step], col_r.at[step], "dp", source)
        arrived(vecs.at[source], vec_s.at[step], vec_r.at[step], "dp", source)
    for g in range(pieces):
        part = pl.ds(g * piece, piece)
        for far in range(1, n_x):
            source = 2 * lax.rem(x + n_x - far, n_x) + 1 - core
            arrived(
                gathered.at[source, part], fwd_s.at[far, g], fwd_r.at[far, g], "dp", partner
            )
    for step in range(1, n_mp):
        source = lax.rem(me + n_mp - step, n_mp)
        arrived(total.at[source], out_s.at[step], out_r.at[step], "mp", source)
    for copy in own:
        copy.wait()
    for copy in sent:
        copy.wait_send()


def exchange(term, block, wide, vec, n_mp, n_dp, collective_id):
    pieces = 2 if block.shape[0] % 32 == 0 else 1
    rows, width = wide.shape[0], wide.shape[1] // n_dp
    dma = pltpu.SemaphoreType.DMA
    chunk = (n_mp, term.shape[0] // n_mp, term.shape[1])
    vmem = pl.BlockSpec(memory_space=pltpu.VMEM)
    total, gathered, columns, vecs = pl.pallas_call(
        functools.partial(exchange_kernel, n_mp, n_dp, pieces),
        out_shape=(
            jax.ShapeDtypeStruct(chunk, term.dtype),
            jax.ShapeDtypeStruct((n_dp,) + block.shape, block.dtype),
            jax.ShapeDtypeStruct((n_dp, rows, width), wide.dtype),
            jax.ShapeDtypeStruct((n_dp,) + vec.shape, vec.dtype),
        ),
        in_specs=[vmem] * 4,
        out_specs=(vmem,) * 4,
        scratch_shapes=[
            pltpu.VMEM(chunk, term.dtype),
            dma((n_mp,)),
            dma((n_mp,)),
            dma((n_mp,)),
            dma((n_mp,)),
            dma((n_dp,)),
            dma((n_dp,)),
            dma((n_dp,)),
            dma((n_dp,)),
            dma,
            dma,
            dma((n_dp // 2, pieces)),
            dma((n_dp // 2, pieces)),
            dma((n_dp // 2, pieces)),
            dma((n_dp // 2, pieces)),
            dma((3,)),
        ],
        compiler_params=pltpu.CompilerParams(
            collective_id=collective_id, has_side_effects=True, vmem_limit_bytes=20 << 20
        ),
    )(term.reshape(chunk), block, wide, vec)
    return (
        total.reshape(term.shape),
        gathered.reshape(n_dp * block.shape[0], block.shape[1]),
        columns.reshape(n_dp * rows, width),
        vecs,
    )


def body(n_mp, n_dp, embeddings, w_in, w_out, means, precisions, log_weight):
    contract_rows = (((0,), (0,)), ((), ()))
    contract_cols = (((1,), (1,)), ((), ()))
    pre = jnp.dot(embeddings, w_in, preferred_element_type=jnp.float32)
    hidden = jax.nn.silu(pre).astype(jnp.bfloat16)
    partial_value = jnp.dot(hidden, w_out, preferred_element_type=jnp.float32)
    spare = jnp.zeros((1, 128), jnp.float32)
    head, hidden_all, emb_cols, _ = exchange(
        partial_value.astype(jnp.bfloat16), hidden, embeddings, spare, n_mp, n_dp, 0
    )
    head_f = head.astype(jnp.float32)
    squares = (head_f * head_f).astype(jnp.bfloat16)
    means_f = means.astype(jnp.float32)
    prec_f = precisions.astype(jnp.float32)
    weighted = (means_f * prec_f).astype(jnp.bfloat16)
    offset = (
        log_weight
        + 0.5 * jnp.sum(jnp.log(prec_f), axis=1)
        - 0.5 * jnp.sum(means_f * means_f * prec_f, axis=1)
    )
    scores = offset[None, :] + lax.dot_general(
        head, weighted, contract_cols, preferred_element_type=jnp.float32
    )
    scores = scores - 0.5 * lax.dot_general(
        squares, precisions, contract_cols, preferred_element_type=jnp.float32
    )
    local_top = jnp.max(scores, axis=1)
    local_total = jnp.sum(jnp.exp(scores - local_top[:, None]), axis=1)
    stats = gather_stats(jnp.stack([local_top, local_total]), n_mp, 1)
    top = jnp.max(stats[:, 0], axis=0)
    total = jnp.sum(stats[:, 1] * jnp.exp(stats[:, 0] - top), axis=0)
    lse = top + jnp.log(total)
    resp = jnp.exp(scores - lse[:, None])
    resp_b = resp.astype(jnp.bfloat16)
    along = jnp.dot(resp_b, precisions, preferred_element_type=jnp.float32)
    shifted = jnp.dot(resp_b, weighted, preferred_element_type=jnp.float32)
    grad_term = head_f * along - shifted
    grad_head, resp_all, head_cols, counts_all = exchange(
        grad_term.astype(jnp.bfloat16),
        resp_b,
        head,
        jnp.sum(resp, axis=0, keepdims=True),
        n_mp,
        n_dp,
        2,
    )
    counts = jnp.sum(counts_all, axis=(0, 1))
    head_cols_f = head_cols.astype(jnp.float32)
    squares_cols = (head_cols_f * head_cols_f).astype(jnp.bfloat16)
    first_moment = lax.dot_general(
        head_cols, resp_all, contract_rows, preferred_element_type=jnp.float32
    )
    second_moment = lax.dot_general(
        squares_cols, resp_all, contract_rows, preferred_element_type=jnp.float32
    )
    back = lax.dot_general(grad_head, w_out, contract_cols, preferred_element_type=jnp.float32)
    sigma = jax.nn.sigmoid(pre)
    grad_pre = (back * sigma * (1.0 + pre * (1.0 - sigma))).astype(jnp.bfloat16)
    embed_term = lax.dot_general(grad_pre, w_in, contract_cols, preferred_element_type=jnp.float32)
    grad_embed, pre_all, grad_cols, _ = exchange(
        embed_term.astype(jnp.bfloat16), grad_pre, grad_head, spare, n_mp, n_dp, 3
    )
    grad_w_in = lax.dot_general(
        emb_cols, pre_all, contract_rows, preferred_element_type=jnp.float32
    ).astype(jnp.bfloat16)
    grad_w_out_t = lax.dot_general(
        grad_cols, hidden_all, contract_rows, preferred_element_type=jnp.float32
    ).astype(jnp.bfloat16)
    return (counts, first_moment, second_moment, grad_w_in, grad_w_out_t, grad_embed)


def solution(mesh):
    return jax.shard_map(
        functools.partial(body, mesh.shape["mp"], mesh.shape["dp"]),
        mesh=mesh,
        in_specs=(
            P(("parts", "dp"), None),
            P(None, "mp"),
            P("mp", None),
            P("mp", None),
            P("mp", None),
            P("mp"),
        ),
        out_specs=(
            P(("parts", "mp")),
            P(("parts", "dp"), "mp"),
            P(("parts", "dp"), "mp"),
            P(("parts", "dp"), "mp"),
            P(("parts", "dp"), "mp"),
            P(("parts", "dp"), None),
        ),
        check_vma=False,
    )
```
